32 devices in a mesh: str: 8 (over z, x), fac: 4 (over y, core).
Axes of the slice: x: 2, y: 2, z: 4, core: 2. Of those that a mesh axis runs over, the one named last changes fastest.
Arguments:
- amplitudes: bfloat16 [2, 4096, 4096], P(None, 'str'), may hold values from -6 to 6
- beta_index: int32 [2, 32, 12], replicated, may hold values from 0 to 31, all different within a row; in each aligned block of 32 rows (0 to 31, 32 to 63, ..., all dimensions but the last counted through in order) at most 24 rows name the same one
- beta_tile: int32 [2, 12], replicated, may hold values from 0 to 15
- beta_flip: int32 [2, 4096], replicated, may hold values 0 or 1
- alpha_index: int32 [2, 32, 12], replicated, may hold values from 0 to 31, all different within a row; in each aligned block of 32 rows (0 to 31, 32 to 63, ..., all dimensions but the last counted through in order) at most 24 rows name the same one
- alpha_tile: int32 [2, 12], replicated, may hold values from 0 to 15
- alpha_flip: int32 [2, 4096], replicated, may hold values 0 or 1
- beta_tiles: bfloat16 [16, 128, 128], replicated, may hold values from -0.15625 to 0.15625
- alpha_tiles: bfloat16 [16, 128, 128], replicated, may hold values from -0.109375 to 0.109375
Outputs:
- sigma: float32 [2, 4096, 4096], P(None, 'fac', 'str')
The draws below stay inside these ranges and needn't reach their ends.
Inputs may be any that keep to these rules, and one draw needn't show every extreme that they name: `beta_index`: each block row of one factor's beta operator names 12 different block columns; within one factor's operator no block column is named by more than 24 block rows, and in some factor one column is named by exactly 24. `alpha_index`: each block row of one factor's alpha operator names 12 different block columns; within one factor's operator no block column is named by more than 24 block rows, and in some factor one column is named by exactly 24.
All inputs are finite; a program needn't handle non-finite values.
Results may differ from the reference program's by a relative error of at most 0.012.
Values may be sent and summed in bfloat16 or wider, within the bound.
A program may use at most 128 MiB of HBM per device.

```python
import math
import jax
import jax.numpy as jnp
import numpy as np
from jax import lax

STRINGS = 4096
TILE = 128
KSLOT = 12
NTILE = 16
MOSTREF = 24
NBLK = 32
NFAC = 2


def set_ends(array, key, least, top_value):
    place = [jax.random.randint(jax.random.fold_in(key, axis), (), 0, length) for axis, length in enumerate(array.shape)]
    main_axis = array.shape.index(max(array.shape))
    beside = place[:main_axis] + [(place[main_axis] + 1) % array.shape[main_axis]] + place[main_axis + 1:]
    return array.at[tuple(place)].set(least).at[tuple(beside)].set(top_value)


def shard_levels(stream_key, dims, cuts, least, top_value):
    factor_of, own = 1.0, jax.random.fold_in(stream_key, 6)
    for axis_at, blocks in cuts:
        steps = jnp.exp(jax.random.uniform(jax.random.fold_in(own, axis_at), (blocks,), jnp.float32, least / len(cuts), top_value / len(cuts)))
        factor_of = factor_of * jnp.repeat(steps, dims[axis_at] // blocks).reshape([-1 if axis == axis_at else 1 for axis in range(len(dims))])
    return factor_of


def shared_out(key, own, number, rows, number_of, top, most, lean):
    order = jax.random.permutation(key, number_of)
    packed, ordinary = portions_of(number_of, rows * top, most, lean, True), portions_of(number_of, rows * top, most, lean, False)
    places = jnp.arange(number_of)

    def named(sizes, offset_by):
        used = int((sizes > 0).sum())
        fixed = max(1, used // 4)
        shifted = fixed + (places - fixed + offset_by * (used - fixed)) % max(1, number_of - fixed)
        return jnp.zeros((number_of,), jnp.int32).at[order[jnp.where(places < fixed, places, shifted)]].set(jnp.asarray(sizes, jnp.int32))

    sizes = jnp.where(number % 4 == 0, named(packed, number // 4), named(ordinary, number - number // 4 - 1))
    mixed = jax.random.permutation(jax.random.fold_in(own, 3), number_of)
    giver, receiver = mixed[0:number_of // 2 * 2:2], mixed[1:number_of // 2 * 2:2]
    slack = jnp.minimum(sizes[giver] - 1, most - sizes[receiver]) // 2
    slack = jnp.where((giver == order[0]) | (receiver == order[0]) | (sizes[receiver] == 0), 0, jnp.maximum(slack, 0))
    shifted = jax.random.randint(jax.random.fold_in(own, 4), (number_of // 2,), 0, 1 << 20) % (slack + 1)
    sizes = sizes.at[giver].add(-shifted).at[receiver].add(shifted)
    members = jnp.searchsorted(jnp.cumsum(sizes), jnp.arange(rows * top), side="right").astype(jnp.int32)
    listing = members.reshape(top, rows).T
    listing = listing[jax.random.permutation(jax.random.fold_in(own, 1), rows)]
    offset_by = jax.random.randint(jax.random.fold_in(own, 2), (rows, 1), 0, top)
    return jnp.take_along_axis(listing, (jnp.arange(top)[None, :] + offset_by) % top, axis=1)


def portions_of(count, total, limit, skew, full):
    weights = [(1 << 20) // math.isqrt(standing ** skew) + 1 for standing in range(1, count + 1)]
    largest = limit if full else min(limit, max(-(-total // count), total * weights[0] // sum(weights)))
    least = 1 if total - largest >= count - 1 else 0
    counts, surplus = [largest] + [least] * (count - 1), total - largest - least * (count - 1)
    while surplus > 0:
        free = [i for i in range(1, count) if counts[i] < largest] or [i for i in range(1, count) if counts[i] < limit]
        pool, budget = sum([weights[i] for i in free]), surplus
        for i in free:
            extra = min(limit - counts[i], max(1, budget * weights[i] // pool), surplus)
            counts[i] = counts[i] + extra
            surplus = surplus - extra
    return np.array(counts)


def scatter_about(rng, shape, scale, reach, cuts=(), held_as=jnp.bfloat16):
    level = shard_levels(rng, shape, cuts, -0.22, 0.18) if cuts else 1.0
    values = jax.random.normal(rng, shape, jnp.float32) * scale * level
    return jnp.minimum(jnp.maximum(values, -reach), reach).astype(held_as)


def setup_inputs(seed: int = 0) -> dict:
    keys = jax.random.split(jax.random.key(seed), 10)
    amplitudes = scatter_about(keys[0], (2, STRINGS, STRINGS), 1.0, 6.0, ((1, 8),))
    beta_index_keys = jax.random.split(jax.random.fold_in(keys[1], 1), NFAC * NBLK // NBLK)
    beta_index_turns = jax.random.permutation(jax.random.fold_in(keys[1], 3), NFAC * NBLK // NBLK)
    beta_index = jax.vmap(lambda own, number: shared_out(jax.random.fold_in(keys[1], 2), own, number, NBLK, NBLK, KSLOT, MOSTREF, 2))(beta_index_keys, beta_index_turns).reshape((NFAC, NBLK, KSLOT))
    beta_tile = set_ends(jax.random.randint(keys[2], (NFAC, KSLOT), 0, NTILE), jax.random.fold_in(keys[2], 1), 0, NTILE - 1).astype(jnp.int32)
    beta_flip = set_ends((jax.random.randint(keys[3], (NFAC, STRINGS), 0, 2) < 1).astype(jnp.int32), jax.random.fold_in(keys[3], 1), 0, 1)
    alpha_index_keys = jax.random.split(jax.random.fold_in(keys[4], 1), NFAC * NBLK // NBLK)
    alpha_index_turns = jax.random.permutation(jax.random.fold_in(keys[4], 3), NFAC * NBLK // NBLK)
    alpha_index = jax.vmap(lambda own, number: shared_out(jax.random.fold_in(keys[4], 2), own, number, NBLK, NBLK, KSLOT, MOSTREF, 2))(alpha_index_keys, alpha_index_turns).reshape((NFAC, NBLK, KSLOT))
    alpha_tile = set_ends(jax.random.randint(keys[5], (NFAC, KSLOT), 0, NTILE), jax.random.fold_in(keys[5], 1), 0, NTILE - 1).astype(jnp.int32)
    alpha_flip = set_ends((jax.random.randint(keys[6], (NFAC, STRINGS), 0, 2) < 1).astype(jnp.int32), jax.random.fold_in(keys[6], 1), 0, 1)
    beta_tiles = scatter_about(keys[7], (NTILE, TILE, TILE), (TILE * KSLOT) ** -0.5, 0.15625)
    alpha_tiles = scatter_about(keys[8], (NTILE, TILE, TILE), (TILE * KSLOT * NFAC) ** -0.5, 0.109375)
    return {"amplitudes": amplitudes, "beta_index": beta_index, "beta_tile": beta_tile, "beta_flip": beta_flip, "alpha_index": alpha_index, "alpha_tile": alpha_tile, "alpha_flip": alpha_flip, "beta_tiles": beta_tiles, "alpha_tiles": alpha_tiles}


def apply_beta(amplitudes, block_ids, tile_ids, flips, tile_table):
    part_count, height, column_count = amplitudes.shape
    tile_size = tile_table.shape[1]
    block_count = column_count // tile_size
    signs = (1 - 2 * flips).astype(jnp.bfloat16)
    signed = amplitudes * signs[None, None, :]
    blocks = signed.reshape(part_count, height, block_count, tile_size)
    weights = tile_table[tile_ids].astype(jnp.float32)
    group_size = block_count // 4
    pieces = []
    for group_id in range(4):
        lower = group_id * group_size
        chosen = block_ids[lower:lower + group_size]
        gathered = blocks[:, :, chosen].astype(jnp.float32)
        pieces.append(jnp.einsum("pajkc,krc->pajr", gathered, weights).astype(jnp.bfloat16))
    return jnp.concatenate(pieces, axis=2).reshape(part_count, height, column_count)


def apply_alpha(half, block_ids, tile_ids, flips, tile_table):
    part_count, total, column_count = half.shape
    tile_size = tile_table.shape[1]
    block_count = total // tile_size
    signs = (1 - 2 * flips).astype(jnp.bfloat16)
    signed = half * signs[None, :, None]
    blocks = signed.reshape(part_count, block_count, tile_size, column_count)
    weights = tile_table[tile_ids].astype(jnp.float32)
    group_size = block_count // 4
    pieces = []
    for group_id in range(4):
        lower = group_id * group_size
        chosen = block_ids[lower:lower + group_size]
        gathered = blocks[:, chosen].astype(jnp.float32)
        pieces.append(jnp.einsum("pjkcn,krc->pjrn", gathered, weights).astype(jnp.bfloat16))
    return jnp.concatenate(pieces, axis=1).reshape(part_count, total, column_count)


def reference(amplitudes, beta_index, beta_tile, beta_flip, alpha_index, alpha_tile, alpha_flip, beta_tiles, alpha_tiles):
    def accumulate(factor, summed):
        half = apply_beta(amplitudes, beta_index[factor], beta_tile[factor], beta_flip[factor], beta_tiles)
        half = lax.optimization_barrier(half)
        rounded = apply_alpha(half, alpha_index[factor], alpha_tile[factor], alpha_flip[factor], alpha_tiles)
        rounded = lax.optimization_barrier(rounded)
        return summed + rounded.astype(jnp.float32)

    initial = jnp.zeros(amplitudes.shape, jnp.float32)
    return lax.fori_loop(0, NFAC, accumulate, initial)
```

```python
import functools

import jax
import jax.numpy as jnp
from jax import lax
from jax.experimental import pallas as pl
from jax.experimental.pallas import tpu as pltpu
from jax.sharding import PartitionSpec as P

MESH = pl.DeviceIdType.MESH


def kernel(dims, amp_hbm, sign_b, sign_a, bidx, btile, aidx, atile, btab, atab, out, *scratch):
    S, F, NF, C, A, T, K = dims
    amp, half_send, term_send, wb, wa = scratch[:5]
    recv = scratch[5 : 5 + C]
    a_sem, s_send, s_recv, f_send, f_recv = scratch[5 + C :]
    me = lax.axis_index("str")
    pos = lax.axis_index("fac")
    fac = pos // 2
    part = pos % 2
    rows = A * T
    per = term_send.shape[1] // F

    def load(k):
        return pltpu.make_async_copy(amp_hbm.at[part, :, pl.ds(pl.multiple_of(k * T, T), T)], amp.at[k], a_sem.at[k])

    def start_load(k, _):
        load(k).start()
        return 0

    NB = amp.shape[0]
    lax.fori_loop(0, NB, start_load, 0)

    barrier = pltpu.get_barrier_semaphore()

    def greet_str(t, _):
        pl.semaphore_signal(barrier, inc=1, device_id={"str": (me + 1 + t) % S}, device_id_type=MESH)
        return 0

    def greet_fac(t, _):
        pl.semaphore_signal(barrier, inc=1, device_id={"fac": (pos + 1 + t) % F}, device_id_type=MESH)
        return 0

    lax.fori_loop(0, S - 1, greet_str, 0)
    lax.fori_loop(0, F - 1, greet_fac, 0)

    for s in range(K):
        wb[pl.ds(s * T, T), :] = btab[btile[fac, s]].T
        wa[:, pl.ds(s * T, T)] = atab[atile[fac, s]]

    def sign(k, _):
        load(k).wait()
        amp[k] = amp[k] * sign_b[k] * sign_a[...]
        return 0

    lax.fori_loop(0, NB, sign, 0)
    pl.semaphore_wait(barrier, S + F - 2)

    mid = S // 2

    def dest(t):
        side = (me // mid + 1 + t // mid) % 2
        return side * mid + (me + 1 + t) % mid

    def beta(q, c):
        j = q * C + c
        lhs = jnp.concatenate([amp[bidx[fac, j, s]] for s in range(K)], axis=1)
        res = jnp.dot(lhs, wb[...], preferred_element_type=jnp.float32)
        return res.astype(jnp.bfloat16).reshape(A, T, T)

    def str_copy(c, q, src):
        return pltpu.make_async_remote_copy(
            src_ref=half_send.at[c, q],
            dst_ref=recv[c].at[pl.ds(src * A, A)],
            send_sem=s_send.at[c, q],
            recv_sem=s_recv.at[c, src],
            device_id={"str": q},
            device_id_type=MESH,
        )

    for c in range(C):

        def step(t, _):
            q = dest(t)
            half_send[c, q] = beta(q, c)
            str_copy(c, q, me).start()
            return 0

        lax.fori_loop(0, S - 1, step, 0)
        recv[c][pl.ds(me * A, A)] = beta(me, c)

    def fac_target(g):
        return ((fac + 1 + g // 2) % NF) * 2 + (part + 1 + g % 2) % 2

    def fac_copy(c, p, src_fac, src_part):
        return pltpu.make_async_remote_copy(
            src_ref=term_send.at[c, pl.ds(p * per, per)],
            dst_ref=out.at[src_fac, src_part, :, pl.ds(c * T, T)],
            send_sem=f_send.at[c, p],
            recv_sem=f_recv.at[c, src_fac * 2 + src_part],
            device_id={"fac": p},
            device_id_type=MESH,
        )

    def own_copy(c):
        return pltpu.make_async_copy(
            term_send.at[c, pl.ds(pos * per, per)],
            out.at[fac, part, :, pl.ds(c * T, T)],
            f_send.at[c, pos],
        )

    for c in range(C):

        def arrive(t, _):
            src = (me + 1 + t) % S
            str_copy(c, src, src).wait_recv()
            return 0

        lax.fori_loop(0, S - 1, arrive, 0)

        def rows_of(p):
            def block(b, _):
                i = p * (per // T) + b
                rhs = jnp.concatenate([recv[c][aidx[fac, i, s]] for s in range(K)], axis=0)
                res = jnp.dot(wa[...], rhs, preferred_element_type=jnp.float32)
                term_send[c, pl.ds(pl.multiple_of(i * T, T), T), :] = res.astype(jnp.bfloat16)
                return 0

            lax.fori_loop(0, per // T, block, 0)

        def group(g, _):
            p = fac_target(g)
            rows_of(p)
            fac_copy(c, p, fac, part).start()
            return 0

        lax.fori_loop(0, F - 1, group, 0)
        rows_of(pos)
        own_copy(c).start()

    for c in range(C):

        def finish_str(t, _):
            q = (me + 1 + t) % S
            str_copy(c, q, me).wait_send()
            return 0

        lax.fori_loop(0, S - 1, finish_str, 0)

        def finish_fac(t, _):
            p = (pos + 1 + t) % F
            fac_copy(c, p, fac, part).wait_send()
            fac_copy(c, p, p // 2, p % 2).wait_recv()
            return 0

        lax.fori_loop(0, F - 1, finish_fac, 0)
        own_copy(c).wait()


def local(S, F, amplitudes, beta_index, beta_tile, beta_flip, alpha_index, alpha_tile, alpha_flip, beta_tiles, alpha_tiles):
    NF, NB, K = beta_index.shape
    T = beta_tiles.shape[1]
    parts, height, width = amplitudes.shape
    total = height * S
    A = height // T
    C = width // S // T
    pos = lax.axis_index("fac")
    me = lax.axis_index("str")
    bflip = lax.dynamic_index_in_dim(beta_flip, pos // 2, 0, keepdims=False)
    aflip = lax.dynamic_slice(alpha_flip, (pos // 2, me * height), (1, height))[0]
    sign_b = (1 - 2 * bflip).astype(jnp.bfloat16).reshape(NB, 1, T)
    sign_a = jnp.broadcast_to((1 - 2 * aflip).astype(jnp.bfloat16)[:, None], (height, T))
    dims = (S, F, NF, C, A, T, K)
    vmem = pl.BlockSpec(memory_space=pltpu.VMEM)
    smem = pl.BlockSpec(memory_space=pltpu.SMEM)
    terms = pl.pallas_call(
        functools.partial(kernel, dims),
        out_shape=jax.ShapeDtypeStruct((NF, parts, total // F, width // S), jnp.bfloat16),
        in_specs=[pl.BlockSpec(memory_space=pl.ANY), vmem, vmem, smem, smem, smem, smem, vmem, vmem],
        out_specs=pl.BlockSpec(memory_space=pl.ANY),
        scratch_shapes=[
            pltpu.VMEM((NB, height, T), jnp.bfloat16),
            pltpu.VMEM((C, S, A, T, T), jnp.bfloat16),
            pltpu.VMEM((C, total, T), jnp.bfloat16),
            pltpu.VMEM((K * T, T), jnp.bfloat16),
            pltpu.VMEM((T, K * T), jnp.bfloat16),
        ]
        + [pltpu.VMEM((NB, T, T), jnp.bfloat16) for _ in range(C)]
        + [
            pltpu.SemaphoreType.DMA((NB,)),
            pltpu.SemaphoreType.DMA((C, S)),
            pltpu.SemaphoreType.DMA((C, S)),
            pltpu.SemaphoreType.DMA((C, F)),
            pltpu.SemaphoreType.DMA((C, F)),
        ],
        compiler_params=pltpu.CompilerParams(collective_id=0, has_side_effects=True, vmem_limit_bytes=48 * 1024 * 1024),
        name="sigma",
    )(amplitudes, sign_b, sign_a, beta_index, beta_tile, alpha_index, alpha_tile, beta_tiles, alpha_tiles)
    return jnp.sum(terms.astype(jnp.float32), axis=0)


def solution(mesh):
    return jax.shard_map(
        functools.partial(local, mesh.shape["str"], mesh.shape["fac"]),
        mesh=mesh,
        in_specs=(P(None, "str", None), P(), P(), P(), P(), P(), P(), P(), P()),
        out_specs=P(None, "fac", "str"),
        check_vma=False,
    )
```

```python
import functools

import jax
import jax.numpy as jnp
from jax import lax
from jax.experimental import pallas as pl
from jax.experimental.pallas import tpu as pltpu
from jax.sharding import PartitionSpec as P

MESH = pl.DeviceIdType.MESH


def split_position(pos, F):
    factors = F // 2
    return pos % factors, pos // factors


def kernel(dims, amp_hbm, bflip_hbm, aflip_hbm, btab_hbm, atab_hbm, ids, out, *scratch):
    S, F, C, A, T, K, NB = dims
    amp, half_send, term_send, pair_recv, wb, wa, bflip, aflip, btab, atab, sign_a = scratch[:11]
    recv = scratch[11 : 11 + C]
    a_sem, t_sem, s_send, s_recv, p_send, p_recv, f_send, f_recv = scratch[11 + C :]
    me = lax.axis_index("str")
    pos = lax.axis_index("fac")
    fac, part = split_position(pos, F)
    chips = F // 2
    chip = pos // 2
    core = pos % 2
    per = term_send.shape[1] // F

    barrier = pltpu.get_barrier_semaphore()

    def greet_str(t, _):
        pl.semaphore_signal(barrier, inc=1, device_id={"str": (me + 1 + t) % S}, device_id_type=MESH)
        return 0

    def greet_fac(t, _):
        peer = ((chip + 1 + t) % chips) * 2 + core
        pl.semaphore_signal(barrier, inc=1, device_id={"fac": peer}, device_id_type=MESH)
        return 0

    partner = chip * 2 + 1 - core
    lax.fori_loop(0, S - 1, greet_str, 0)
    lax.fori_loop(0, chips - 1, greet_fac, 0)
    pl.semaphore_signal(barrier, inc=1, device_id={"fac": partner}, device_id_type=MESH)

    tables = [
        pltpu.make_async_copy(src, dst, t_sem.at[n])
        for n, (src, dst) in enumerate([(bflip_hbm, bflip), (aflip_hbm, aflip), (btab_hbm, btab), (atab_hbm, atab)])
    ]

    def load(k):
        return pltpu.make_async_copy(amp_hbm.at[part, :, pl.ds(pl.multiple_of(k * T, T), T)], amp.at[k], a_sem.at[k])

    def start_load(k, _):
        load(k).start()
        return 0

    for copy in tables[:3]:
        copy.start()
    lax.fori_loop(0, NB, start_load, 0)
    tables[3].start()

    def signs(flips, block):
        value = flips[:, pl.ds(pl.multiple_of(block * T, T), T)].astype(jnp.float32)
        mine = lax.broadcasted_iota(jnp.int32, value.shape, 0) == fac
        return 1 - 2 * jnp.sum(jnp.where(mine, value, 0.0), axis=0, keepdims=True)

    tables[1].wait()
    for r in range(A):
        row = signs(aflip, me * A + r)
        sign_a[pl.ds(r * T, T), :] = jnp.broadcast_to(row, (T, T)).T.astype(jnp.bfloat16)
    tables[2].wait()
    for s in range(K):
        wb[pl.ds(s * T, T), :] = btab[ids[2 * K, s]].T
    tables[0].wait()

    def sign(k, _):
        load(k).wait()
        amp[k] = amp[k] * signs(bflip, k).astype(jnp.bfloat16) * sign_a[...]
        return 0

    lax.fori_loop(0, NB, sign, 0)
    pl.semaphore_wait(barrier, S - 1 + chips)

    mid = S // 2

    def dest(t):
        side = (me // mid + 1 + t // mid) % 2
        return side * mid + (me + 1 + t) % mid

    def beta(q, c):
        j = q * C + c
        lhs = jnp.concatenate([amp[ids[s, j]] for s in range(K)], axis=1)
        res = jnp.dot(lhs, wb[...], preferred_element_type=jnp.float32)
        return res.astype(jnp.bfloat16).reshape(A, T, T)

    def str_copy(c, q, src):
        return pltpu.make_async_remote_copy(
            src_ref=half_send.at[c, q],
            dst_ref=recv[c].at[pl.ds(src * A, A)],
            send_sem=s_send.at[c, q],
            recv_sem=s_recv.at[c, src],
            device_id={"str": q},
            device_id_type=MESH,
        )

    for c in range(C):

        def step(t, _):
            q = dest(t)
            half_send[c, q] = beta(q, c)
            str_copy(c, q, me).start()
            return 0

        lax.fori_loop(0, S - 1, step, 0)
        recv[c][pl.ds(me * A, A)] = beta(me, c)

    tables[3].wait()
    for s in range(K):
        wa[:, pl.ds(s * T, T)] = atab[ids[2 * K + 1, s]]

    def pair_copy(c, y, owner):
        return pltpu.make_async_remote_copy(
            src_ref=term_send.at[c, pl.ds((y * 2 + owner) * per, per)],
            dst_ref=pair_recv.at[c, y],
            send_sem=p_send.at[c, y],
            recv_sem=p_recv.at[c, y],
            device_id={"fac": partner},
            device_id_type=MESH,
        )

    def fac_copy(c, y, src):
        src_fac, src_part = split_position(src, F)
        return pltpu.make_async_remote_copy(
            src_ref=term_send.at[c, pl.ds((y * 2 + core) * per, per)],
            dst_ref=out.at[src_fac // 2, src_part, :, pl.ds(c * T, T)],
            send_sem=f_send.at[c, y],
            recv_sem=f_recv.at[c, src // 2],
            device_id={"fac": y * 2 + core},
            device_id_type=MESH,
        )

    def own_copy(c):
        return pltpu.make_async_copy(
            term_send.at[c, pl.ds(pos * per, per)],
            out.at[fac // 2, part, :, pl.ds(c * T, T)],
            f_send.at[c, chip],
        )

    for c in range(C):

        def arrive(t, _):
            src = (me + 1 + t) % S
            str_copy(c, src, src).wait_recv()
            return 0

        lax.fori_loop(0, S - 1, arrive, 0)

        def alpha(i):
            rhs = jnp.concatenate([recv[c][ids[K + s, i]] for s in range(K)], axis=0)
            return jnp.dot(wa[...], rhs, preferred_element_type=jnp.float32)

        def store(i, value):
            term_send[c, pl.ds(pl.multiple_of(i * T, T), T), :] = value.astype(jnp.bfloat16)

        def for_partner(y):
            def block(b, _):
                i = (y * 2 + 1 - core) * (per // T) + b
                store(i, alpha(i))
                return 0

            lax.fori_loop(0, per // T, block, 0)
            pair_copy(c, y, 1 - core).start()

        def for_self(y):
            pair_copy(c, y, core).wait_recv()

            def block(b, _):
                i = (y * 2 + core) * (per // T) + b
                other = pair_recv[c, y, pl.ds(pl.multiple_of(b * T, T), T), :]
                store(i, alpha(i) + other.astype(jnp.float32))
                return 0

            lax.fori_loop(0, per // T, block, 0)

        def group(g, _):
            y = (chip + 1 + g) % chips
            for_partner(y)
            for_self(y)
            fac_copy(c, y, pos).start()
            return 0

        lax.fori_loop(0, chips - 1, group, 0)
        for_partner(chip)
        for_self(chip)
        own_copy(c).start()

    for c in range(C):

        def finish_str(t, _):
            str_copy(c, (me + 1 + t) % S, me).wait_send()
            return 0

        lax.fori_loop(0, S - 1, finish_str, 0)

        def finish_pair(y, _):
            pair_copy(c, y, 1 - core).wait_send()
            return 0

        lax.fori_loop(0, chips, finish_pair, 0)

        def finish_fac(t, _):
            y = (chip + 1 + t) % chips
            fac_copy(c, y, pos).wait_send()
            fac_copy(c, y, y * 2 + core).wait_recv()
            return 0

        lax.fori_loop(0, chips - 1, finish_fac, 0)
        own_copy(c).wait()


def local(S, F, amplitudes, beta_index, beta_tile, beta_flip, alpha_index, alpha_tile, alpha_flip, beta_tiles, alpha_tiles):
    NF, NB, K = beta_index.shape
    NT, T, _ = beta_tiles.shape
    parts, height, width = amplitudes.shape
    total = height * S
    A = height // T
    C = width // S // T
    assert F == 2 * NF and parts == 2 and NF % 2 == 0 and K <= NB
    per = total // F
    fac, _ = split_position(lax.axis_index("fac"), F)
    lists = [lax.dynamic_index_in_dim(x.transpose(2, 0, 1), fac, 1, keepdims=False) for x in (beta_index, alpha_index)]
    kinds = [lax.dynamic_slice(x, (fac, 0), (1, K)) for x in (beta_tile, alpha_tile)]
    ids = jnp.concatenate(lists + [jnp.pad(x, ((0, 0), (0, NB - K))) for x in kinds], axis=0)
    hbm = pl.BlockSpec(memory_space=pl.ANY)
    bf16 = jnp.bfloat16
    dma = pltpu.SemaphoreType.DMA
    terms = pl.pallas_call(
        functools.partial(kernel, (S, F, C, A, T, K, NB)),
        out_shape=jax.ShapeDtypeStruct((NF // 2, parts, per, width // S), bf16),
        in_specs=[hbm] * 5 + [pl.BlockSpec(memory_space=pltpu.SMEM)],
        out_specs=hbm,
        scratch_shapes=[
            pltpu.VMEM((NB, height, T), bf16),
            pltpu.VMEM((C, S, A, T, T), bf16),
            pltpu.VMEM((C, total, T), bf16),
            pltpu.VMEM((C, F // 2, per, T), bf16),
            pltpu.VMEM((K * T, T), bf16),
            pltpu.VMEM((T, K * T), bf16),
            pltpu.VMEM((NF, width), jnp.int32),
            pltpu.VMEM((NF, total), jnp.int32),
            pltpu.VMEM((NT, T, T), bf16),
            pltpu.VMEM((NT, T, T), bf16),
            pltpu.VMEM((height, T), bf16),
        ]
        + [pltpu.VMEM((NB, T, T), bf16) for _ in range(C)]
        + [dma((NB,)), dma((4,)), dma((C, S)), dma((C, S))]
        + [dma((C, F // 2)) for _ in range(4)],
        compiler_params=pltpu.CompilerParams(collective_id=0, has_side_effects=True, vmem_limit_bytes=67043328),
        name="sigma",
    )(amplitudes, beta_flip, alpha_flip, beta_tiles, alpha_tiles, ids)
    return jnp.sum(terms.astype(jnp.float32), axis=0)


def solution(mesh):
    return jax.shard_map(
        functools.partial(local, mesh.shape["str"], mesh.shape["fac"]),
        mesh=mesh,
        in_specs=(P(None, "str", None), P(), P(), P(), P(), P(), P(), P(), P()),
        out_specs=P(None, "fac", "str"),
        check_vma=False,
    )
```

```python
import functools
import math

import jax
import jax.numpy as jnp
from jax import lax
from jax.experimental import pallas as pl
from jax.experimental.pallas import tpu as pltpu
from jax.sharding import PartitionSpec as P

MESH = pl.DeviceIdType.MESH


def split_position(pos, F):
    factors = F // 2
    return pos % factors, pos // factors


def kernel(dims, amp_hbm, bflip_hbm, aflip_hbm, btab_hbm, atab_hbm, bidx_hbm, aidx_hbm, btile_hbm, atile_hbm, out, *scratch):
    S, F, C, A, T, K, NB, H = dims
    amp, half_send, term_send, pair_recv, wb, wa, bflip, aflip, btab, atab, sign_a, bidx, aidx, btile, atile = scratch[:15]
    recv = scratch[15 : 15 + C]
    a_sem, t_sem, s_send, s_recv, p_send, p_recv, f_send, f_recv = scratch[15 + C :]
    me = lax.axis_index("str")
    pos = lax.axis_index("fac")
    fac, part = split_position(pos, F)
    chips = F // 2
    chip = pos // 2
    core = pos % 2
    per = term_send.shape[1] // F

    barrier = pltpu.get_barrier_semaphore()

    def greet_str(t, _):
        pl.semaphore_signal(barrier, inc=1, device_id={"str": (me + 1 + t) % S}, device_id_type=MESH)
        return 0

    def greet_fac(t, _):
        peer = ((chip + 1 + t) % chips) * 2 + core
        pl.semaphore_signal(barrier, inc=1, device_id={"fac": peer}, device_id_type=MESH)
        return 0

    partner = chip * 2 + 1 - core
    lax.fori_loop(0, S - 1, greet_str, 0)
    lax.fori_loop(0, chips - 1, greet_fac, 0)
    pl.semaphore_signal(barrier, inc=1, device_id={"fac": partner}, device_id_type=MESH)

    tables = [
        pltpu.make_async_copy(src, dst, t_sem.at[n])
        for n, (src, dst) in enumerate(
            [
                (bflip_hbm, bflip),
                (aflip_hbm, aflip),
                (btab_hbm, btab),
                (bidx_hbm, bidx),
                (btile_hbm, btile),
                (atab_hbm, atab),
                (aidx_hbm, aidx),
                (atile_hbm, atile),
            ]
        )
    ]

    def load(k):
        return pltpu.make_async_copy(amp_hbm.at[part, :, pl.ds(pl.multiple_of(k * T, T), T)], amp.at[k], a_sem.at[k])

    def start_load(k, _):
        load(k).start()
        return 0

    for copy in tables[:5]:
        copy.start()
    lax.fori_loop(0, NB, start_load, 0)
    for copy in tables[5:]:
        copy.start()

    def signs(flips, block):
        value = flips[:, pl.ds(pl.multiple_of(block * T, T), T)].astype(jnp.float32)
        mine = lax.broadcasted_iota(jnp.int32, value.shape, 0) == fac
        return 1 - 2 * jnp.sum(jnp.where(mine, value, 0.0), axis=0, keepdims=True)

    tables[1].wait()
    for r in range(A):
        row = signs(aflip, me * A + r)
        sign_a[pl.ds(r * T, T), :] = jnp.broadcast_to(row, (T, T)).T.astype(jnp.bfloat16)
    tables[4].wait()
    tables[2].wait()
    for s in range(K):
        wb[pl.ds(s * T, T), :] = btab[btile[fac, s]].T
    tables[0].wait()
    tables[3].wait()

    def sign(k, _):
        load(k).wait()
        amp[k] = amp[k] * signs(bflip, k).astype(jnp.bfloat16) * sign_a[...]
        return 0

    lax.fori_loop(0, NB, sign, 0)
    pl.semaphore_wait(barrier, S - 1 + chips)

    mid = S // 2

    def dest(t):
        side = (me // mid + 1 + t // mid) % 2
        return side * mid + (me + 1 + t) % mid

    def beta(q, c):
        j = q * C + c
        lhs = jnp.concatenate([amp[bidx[s, fac, j]] for s in range(K)], axis=1)
        res = jnp.dot(lhs, wb[...], preferred_element_type=jnp.float32)
        return res.astype(jnp.bfloat16).reshape(A, T, T)

    def str_copy(c, q, src):
        return pltpu.make_async_remote_copy(
            src_ref=half_send.at[c, q],
            dst_ref=recv[c].at[pl.ds(src * A, A)],
            send_sem=s_send.at[c, q],
            recv_sem=s_recv.at[c, src],
            device_id={"str": q},
            device_id_type=MESH,
        )

    for c in range(C):

        def step(t, _):
            q = dest(t)
            half_send[c, q] = beta(q, c)
            str_copy(c, q, me).start()
            return 0

        lax.fori_loop(0, S - 1, step, 0)
        recv[c][pl.ds(me * A, A)] = beta(me, c)

    for copy in tables[5:]:
        copy.wait()
    for s in range(K):
        wa[:, pl.ds(s * T, T)] = atab[atile[fac, s]]

    piece = per // H
    groups = chips * H

    def place(g):
        return (chip + 1 + g // H) % chips, g % H

    def pair_copy(c, y, h, owner):
        return pltpu.make_async_remote_copy(
            src_ref=term_send.at[c, pl.ds((y * 2 + owner) * per + h * piece, piece)],
            dst_ref=pair_recv.at[c, y, h],
            send_sem=p_send.at[c, y, h],
            recv_sem=p_recv.at[c, y, h],
            device_id={"fac": partner},
            device_id_type=MESH,
        )

    def fac_copy(c, y, h, src):
        src_fac, src_part = split_position(src, F)
        return pltpu.make_async_remote_copy(
            src_ref=term_send.at[c, pl.ds((y * 2 + core) * per + h * piece, piece)],
            dst_ref=out.at[src_fac // 2, src_part, pl.ds(h * piece, piece), pl.ds(c * T, T)],
            send_sem=f_send.at[c, y, h],
            recv_sem=f_recv.at[c, src // 2, h],
            device_id={"fac": y * 2 + core},
            device_id_type=MESH,
        )

    def own_copy(c):
        return pltpu.make_async_copy(
            term_send.at[c, pl.ds(pos * per, per)],
            out.at[fac // 2, part, :, pl.ds(c * T, T)],
            f_send.at[c, chip, 0],
        )

    for c in range(C):

        def arrive(t, _):
            src = (me + 1 + t) % S
            str_copy(c, src, src).wait_recv()
            return 0

        lax.fori_loop(0, S - 1, arrive, 0)

        def alpha(i):
            rhs = jnp.concatenate([recv[c][aidx[s, fac, i]] for s in range(K)], axis=0)
            return jnp.dot(wa[...], rhs, preferred_element_type=jnp.float32)

        def store(i, value):
            term_send[c, pl.ds(pl.multiple_of(i * T, T), T), :] = value.astype(jnp.bfloat16)

        def for_partner(g):
            y, h = place(g)

            def block(b, _):
                i = (y * 2 + 1 - core) * (per // T) + h * (piece // T) + b
                store(i, alpha(i))
                return 0

            lax.fori_loop(0, piece // T, block, 0)
            pair_copy(c, y, h, 1 - core).start()

        def for_self(g):
            y, h = place(g)
            pair_copy(c, y, h, core).wait_recv()

            def block(b, _):
                i = (y * 2 + core) * (per // T) + h * (piece // T) + b
                other = pair_recv[c, y, h, pl.ds(pl.multiple_of(b * T, T), T), :]
                store(i, alpha(i) + other.astype(jnp.float32))
                return 0

            lax.fori_loop(0, piece // T, block, 0)

        def away(g, _):
            for_partner(g + 1)
            for_self(g)
            y, h = place(g)
            fac_copy(c, y, h, pos).start()
            return 0

        def home(g, _):
            for_partner(g + 1)
            for_self(g)
            return 0

        for_partner(0)
        lax.fori_loop(0, groups - H, away, 0)
        lax.fori_loop(groups - H, groups - 1, home, 0)
        for_self(groups - 1)
        own_copy(c).start()

    for c in range(C):

        def finish_str(t, _):
            str_copy(c, (me + 1 + t) % S, me).wait_send()
            return 0

        lax.fori_loop(0, S - 1, finish_str, 0)

        def finish_pair(g, _):
            y, h = place(g)
            pair_copy(c, y, h, 1 - core).wait_send()
            return 0

        lax.fori_loop(0, groups, finish_pair, 0)

        def finish_fac(g, _):
            y, h = place(g)
            fac_copy(c, y, h, pos).wait_send()
            fac_copy(c, y, h, y * 2 + core).wait_recv()
            return 0

        lax.fori_loop(0, groups - H, finish_fac, 0)
        own_copy(c).wait()


def local(S, F, amplitudes, beta_index, beta_tile, beta_flip, alpha_index, alpha_tile, alpha_flip, beta_tiles, alpha_tiles):
    NF, NB, K = beta_index.shape
    NT, T, _ = beta_tiles.shape
    parts, height, width = amplitudes.shape
    total = height * S
    A = height // T
    C = width // S // T
    assert F == 2 * NF and parts == 2 and NF % 2 == 0 and K <= NB
    per = total // F
    H = math.gcd(per // T, 4)
    ids = (beta_index.transpose(2, 0, 1), alpha_index.transpose(2, 0, 1), beta_tile, alpha_tile)
    hbm = pl.BlockSpec(memory_space=pltpu.HBM)
    bf16 = jnp.bfloat16
    dma = pltpu.SemaphoreType.DMA
    terms = pl.pallas_call(
        functools.partial(kernel, (S, F, C, A, T, K, NB, H)),
        out_shape=jax.ShapeDtypeStruct((NF // 2, parts, per, width // S), bf16),
        in_specs=[hbm] * 9,
        out_specs=pl.BlockSpec(memory_space=pl.ANY),
        scratch_shapes=[
            pltpu.VMEM((NB, height, T), bf16),
            pltpu.VMEM((C, S, A, T, T), bf16),
            pltpu.VMEM((C, total, T), bf16),
            pltpu.VMEM((C, F // 2, H, per // H, T), bf16),
            pltpu.VMEM((K * T, T), bf16),
            pltpu.VMEM((T, K * T), bf16),
            pltpu.VMEM((NF, width), jnp.int32),
            pltpu.VMEM((NF, total), jnp.int32),
            pltpu.VMEM((NT, T, T), bf16),
            pltpu.VMEM((NT, T, T), bf16),
            pltpu.VMEM((height, T), bf16),
            pltpu.SMEM((K, NF, NB), jnp.int32),
            pltpu.SMEM((K, NF, NB), jnp.int32),
            pltpu.SMEM((NF, K), jnp.int32),
            pltpu.SMEM((NF, K), jnp.int32),
        ]
        + [pltpu.VMEM((NB, T, T), bf16) for _ in range(C)]
        + [dma((NB,)), dma((8,)), dma((C, S)), dma((C, S))]
        + [dma((C, F // 2, H)) for _ in range(4)],
        compiler_params=pltpu.CompilerParams(collective_id=0, has_side_effects=True, vmem_limit_bytes=67043328),
        name="sigma",
    )(amplitudes, beta_flip, alpha_flip, beta_tiles, alpha_tiles, *ids)
    return jnp.sum(terms.astype(jnp.float32), axis=0)


def solution(mesh):
    return jax.shard_map(
        functools.partial(local, mesh.shape["str"], mesh.shape["fac"]),
        mesh=mesh,
        in_specs=(P(None, "str", None), P(), P(), P(), P(), P(), P(), P(), P()),
        out_specs=P(None, "fac", "str"),
        check_vma=False,
    )
```

```python
import functools
import math

import jax
import jax.numpy as jnp
from jax import lax
from jax.experimental import pallas as pl
from jax.experimental.pallas import tpu as pltpu
from jax.sharding import PartitionSpec as P

MESH = pl.DeviceIdType.MESH


def split_position(pos, F):
    factors = F // 2
    return pos % factors, pos // factors


def kernel(dims, amp_hbm, bflip_hbm, aflip_hbm, btab_hbm, atab_hbm, bidx_hbm, aidx_hbm, btile_hbm, atile_hbm, out, *scratch):
    S, F, C, A, T, K, NB, H = dims
    amp, half_send, term_send, pair_recv, wb, wa, bflip, aflip, btab, atab, sign_a, bidx, aidx, btile, atile, raw = scratch[:16]
    recv = scratch[16 : 16 + C]
    a_sem, t_sem, s_send, s_recv, p_send, p_recv, f_send, f_recv = scratch[16 + C :]
    me = lax.axis_index("str")
    pos = lax.axis_index("fac")
    fac, part = split_position(pos, F)
    chips = F // 2
    chip = pos // 2
    core = pos % 2
    per = term_send.shape[1] // F

    barrier = pltpu.get_barrier_semaphore()

    def greet_str(t, _):
        pl.semaphore_signal(barrier, inc=1, device_id={"str": (me + 1 + t) % S}, device_id_type=MESH)
        return 0

    def greet_fac(t, _):
        peer = ((chip + 1 + t) % chips) * 2 + core
        pl.semaphore_signal(barrier, inc=1, device_id={"fac": peer}, device_id_type=MESH)
        return 0

    partner = chip * 2 + 1 - core
    lax.fori_loop(0, S - 1, greet_str, 0)
    lax.fori_loop(0, chips - 1, greet_fac, 0)
    pl.semaphore_signal(barrier, inc=1, device_id={"fac": partner}, device_id_type=MESH)

    tables = [
        pltpu.make_async_copy(src, dst, t_sem.at[n])
        for n, (src, dst) in enumerate(
            [
                (bflip_hbm, bflip),
                (aflip_hbm, aflip),
                (btab_hbm, btab),
                (bidx_hbm, bidx),
                (btile_hbm, btile),
                (atab_hbm, atab),
                (aidx_hbm, aidx),
                (atile_hbm, atile),
            ]
        )
    ]

    strip = A * T // 8

    def load(k):
        return pltpu.make_async_copy(amp_hbm.at[part, pl.ds(k * strip, strip)], raw.at[pl.ds(k * strip, strip)], a_sem.at[k])

    def start_load(k, _):
        load(k).start()
        return 0

    for copy in tables[:5]:
        copy.start()
    lax.fori_loop(0, 8, start_load, 0)
    for copy in tables[5:]:
        copy.start()

    def signs(flips, block):
        value = flips[:, pl.ds(block * T if isinstance(block, int) else pl.multiple_of(block * T, T), T)].astype(jnp.float32)
        mine = lax.broadcasted_iota(jnp.int32, value.shape, 0) == fac
        return 1 - 2 * jnp.sum(jnp.where(mine, value, 0.0), axis=0, keepdims=True)

    tables[1].wait()
    for r in range(A):
        row = signs(aflip, me * A + r)
        sign_a[pl.ds(r * T, T), :] = jnp.broadcast_to(row, (T, T)).T.astype(jnp.bfloat16)
    tables[4].wait()
    tables[2].wait()
    for s in range(K):
        wb[pl.ds(s * T, T), :] = btab[btile[fac, s]].T
    tables[0].wait()
    tables[3].wait()

    def sign(r, _):
        load(r).wait()
        rows = pl.ds(pl.multiple_of(r * strip, strip), strip)
        row_sign = sign_a[rows, :]
        for k in range(NB):
            amp[k, rows, :] = raw[rows, pl.ds(k * T, T)] * signs(bflip, k).astype(jnp.bfloat16) * row_sign
        return 0

    lax.fori_loop(0, 8, sign, 0)
    pl.semaphore_wait(barrier, S - 1 + chips)

    mid = S // 2

    def dest(t):
        side = (me // mid + 1 + t // mid) % 2
        return side * mid + (me + 1 + t) % mid

    def beta(q, c):
        j = q * C + c
        lhs = jnp.concatenate([amp[bidx[s, fac, j]] for s in range(K)], axis=1)
        res = jnp.dot(lhs, wb[...], preferred_element_type=jnp.float32)
        return res.astype(jnp.bfloat16).reshape(A, T, T)

    def str_copy(c, q, src):
        return pltpu.make_async_remote_copy(
            src_ref=half_send.at[c, q],
            dst_ref=recv[c].at[pl.ds(src * A, A)],
            send_sem=s_send.at[c, q],
            recv_sem=s_recv.at[c, src],
            device_id={"str": q},
            device_id_type=MESH,
        )

    for c in range(C):

        def step(t, _):
            q = dest(t)
            half_send[c, q] = beta(q, c)
            str_copy(c, q, me).start()
            return 0

        lax.fori_loop(0, S - 1, step, 0)
        recv[c][pl.ds(me * A, A)] = beta(me, c)

    for copy in tables[5:]:
        copy.wait()
    for s in range(K):
        wa[:, pl.ds(s * T, T)] = atab[atile[fac, s]]

    piece = per // H
    groups = chips * H

    def place(g):
        return (chip + 1 + g // H) % chips, g % H

    def pair_copy(c, y, h, owner):
        return pltpu.make_async_remote_copy(
            src_ref=term_send.at[c, pl.ds((y * 2 + owner) * per + h * piece, piece)],
            dst_ref=pair_recv.at[c, y, h],
            send_sem=p_send.at[c, y, h],
            recv_sem=p_recv.at[c, y, h],
            device_id={"fac": partner},
            device_id_type=MESH,
        )

    def fac_copy(c, y, h, src):
        src_fac, src_part = split_position(src, F)
        return pltpu.make_async_remote_copy(
            src_ref=term_send.at[c, pl.ds((y * 2 + core) * per + h * piece, piece)],
            dst_ref=out.at[src_fac // 2, src_part, pl.ds(h * piece, piece), pl.ds(c * T, T)],
            send_sem=f_send.at[c, y, h],
            recv_sem=f_recv.at[c, src // 2, h],
            device_id={"fac": y * 2 + core},
            device_id_type=MESH,
        )

    def own_copy(c):
        return pltpu.make_async_copy(
            term_send.at[c, pl.ds(pos * per, per)],
            out.at[fac // 2, part, :, pl.ds(c * T, T)],
            f_send.at[c, chip, 0],
        )

    for c in range(C):

        def arrive(t, _):
            src = (me + 1 + t) % S
            str_copy(c, src, src).wait_recv()
            return 0

        lax.fori_loop(0, S - 1, arrive, 0)

        def alpha(i):
            rhs = jnp.concatenate([recv[c][aidx[s, fac, i]] for s in range(K)], axis=0)
            return jnp.dot(wa[...], rhs, preferred_element_type=jnp.float32)

        def store(i, value):
            term_send[c, pl.ds(pl.multiple_of(i * T, T), T), :] = value.astype(jnp.bfloat16)

        def for_partner(g):
            y, h = place(g)

            def block(b, _):
                i = (y * 2 + 1 - core) * (per // T) + h * (piece // T) + b
                store(i, alpha(i))
                return 0

            lax.fori_loop(0, piece // T, block, 0)
            pair_copy(c, y, h, 1 - core).start()

        def for_self(g):
            y, h = place(g)
            pair_copy(c, y, h, core).wait_recv()

            def block(b, _):
                i = (y * 2 + core) * (per // T) + h * (piece // T) + b
                other = pair_recv[c, y, h, pl.ds(pl.multiple_of(b * T, T), T), :]
                store(i, alpha(i) + other.astype(jnp.float32))
                return 0

            lax.fori_loop(0, piece // T, block, 0)

        def away(g, _):
            for_partner(g + 1)
            for_self(g)
            y, h = place(g)
            fac_copy(c, y, h, pos).start()
            return 0

        def home(g, _):
            for_partner(g + 1)
            for_self(g)
            return 0

        for_partner(0)
        lax.fori_loop(0, groups - H, away, 0)
        lax.fori_loop(groups - H, groups - 1, home, 0)
        for_self(groups - 1)
        own_copy(c).start()

    for c in range(C):

        def finish_str(t, _):
            str_copy(c, (me + 1 + t) % S, me).wait_send()
            return 0

        lax.fori_loop(0, S - 1, finish_str, 0)

        def finish_pair(g, _):
            y, h = place(g)
            pair_copy(c, y, h, 1 - core).wait_send()
            return 0

        lax.fori_loop(0, groups, finish_pair, 0)

        def finish_fac(g, _):
            y, h = place(g)
            fac_copy(c, y, h, pos).wait_send()
            fac_copy(c, y, h, y * 2 + core).wait_recv()
            return 0

        lax.fori_loop(0, groups - H, finish_fac, 0)
        own_copy(c).wait()


def local(S, F, amplitudes, beta_index, beta_tile, beta_flip, alpha_index, alpha_tile, alpha_flip, beta_tiles, alpha_tiles):
    NF, NB, K = beta_index.shape
    NT, T, _ = beta_tiles.shape
    parts, height, width = amplitudes.shape
    total = height * S
    A = height // T
    C = width // S // T
    assert F == 2 * NF and parts == 2 and NF % 2 == 0 and height % 128 == 0
    per = total // F
    H = math.gcd(per // T, 4)
    ids = (beta_index.transpose(2, 0, 1), alpha_index.transpose(2, 0, 1), beta_tile, alpha_tile)
    hbm = pl.BlockSpec(memory_space=pltpu.HBM)
    bf16 = jnp.bfloat16
    dma = pltpu.SemaphoreType.DMA
    terms = pl.pallas_call(
        functools.partial(kernel, (S, F, C, A, T, K, NB, H)),
        out_shape=jax.ShapeDtypeStruct((NF // 2, parts, per, width // S), bf16),
        in_specs=[hbm] * 9,
        out_specs=pl.BlockSpec(memory_space=pl.ANY),
        scratch_shapes=[
            pltpu.VMEM((NB, height, T), bf16),
            pltpu.VMEM((C, S, A, T, T), bf16),
            pltpu.VMEM((C, total, T), bf16),
            pltpu.VMEM((C, F // 2, H, per // H, T), bf16),
            pltpu.VMEM((K * T, T), bf16),
            pltpu.VMEM((T, K * T), bf16),
            pltpu.VMEM((NF, width), jnp.int32),
            pltpu.VMEM((NF, total), jnp.int32),
            pltpu.VMEM((NT, T, T), bf16),
            pltpu.VMEM((NT, T, T), bf16),
            pltpu.VMEM((height, T), bf16),
            pltpu.SMEM((K, NF, NB), jnp.int32),
            pltpu.SMEM((K, NF, NB), jnp.int32),
            pltpu.SMEM((NF, K), jnp.int32),
            pltpu.SMEM((NF, K), jnp.int32),
            pltpu.VMEM((height, width), bf16),
        ]
        + [pltpu.VMEM((NB, T, T), bf16) for _ in range(C)]
        + [dma((8,)), dma((8,)), dma((C, S)), dma((C, S))]
        + [dma((C, F // 2, H)) for _ in range(4)],
        compiler_params=pltpu.CompilerParams(collective_id=0, has_side_effects=True, vmem_limit_bytes=67043328),
        name="sigma",
    )(amplitudes, beta_flip, alpha_flip, beta_tiles, alpha_tiles, *ids)
    return jnp.sum(terms.astype(jnp.float32), axis=0)


def solution(mesh):
    return jax.shard_map(
        functools.partial(local, mesh.shape["str"], mesh.shape["fac"]),
        mesh=mesh,
        in_specs=(P(None, "str", None), P(), P(), P(), P(), P(), P(), P(), P()),
        out_specs=P(None, "fac", "str"),
        check_vma=False,
    )
```
